32 devices in a mesh: section: 4 (over y, x), dp: 8 (over z, core).
Axes of the slice: x: 2, y: 2, z: 4, core: 2. Of those that a mesh axis runs over, the one named last changes fastest.
Arguments:
- saved_states: bfloat16 [4, 2, 128, 2688], P('section', None, 'dp'), may hold values from -64 to 64
- cotangent_in: bfloat16 [4, 128, 2688], P('section', 'dp'), may hold values from -6 to 6
- lengths: int32 [4], P('section'), may hold values from 16 to 128
- gain: bfloat16 [2688], replicated, may hold values from 0.099609375 to 1.8984375
- up_weight: bfloat16 [2688, 9216], P('section', 'dp'), may hold values from -0.125 to 0.125
- down_weight: bfloat16 [9216, 2688], P('dp', 'section'), may hold values from -0.0625 to 0.0625
Outputs:
- cotangent_out: bfloat16 [4, 128, 2688], P('section', 'dp')
- up_gradient: bfloat16 [2688, 9216], P('section', 'dp')
- down_gradient: bfloat16 [9216, 2688], P('dp', 'section')
- gain_gradient: float32 [2688], replicated
The draws below stay inside these ranges and needn't reach their ends.
All inputs are finite; a program needn't handle non-finite values.
Results may differ from the reference program's by a relative error of at most 0.024.
Values may be sent and summed in bfloat16 or wider, within the bound.
No kernel may reach another device: no remote copies, remote signals or barrier semaphores. Data moves between devices by JAX's collectives and lax.ppermute only.
A program may use at most 64 MiB of HBM per device.

```python
import math
import jax
import jax.numpy as jnp
from jax import lax

D = 2688
F = 9216
TOK = 128
MICRO = 2
SECTIONS = 4
HIDDEN_BLOCKS = 8
LAP_TOKENS = 1024


def draw_saved_states(key, part):
    first, second, third = jax.random.split(jax.random.fold_in(key, 11), 3)
    shape = (SECTIONS, MICRO, TOK, D)
    row_scale = jnp.exp(jax.random.uniform(second, (SECTIONS, MICRO, TOK, 1), jnp.float32, 0.0, math.log(10.0)))
    column_scale = jnp.exp(jax.random.uniform(third, (D,), jnp.float32, math.log(0.5), math.log(5.0)))
    base = jax.random.normal(first, shape, jnp.float32)
    return jnp.clip(base * row_scale * column_scale, -64.0, 64.0).astype(jnp.bfloat16)


def draw_lengths(key, part):
    first, second, third = jax.random.split(jax.random.fold_in(key, 23), 3)
    values = jax.random.randint(first, (SECTIONS,), TOK // 8, TOK + 1)
    highest = jax.random.randint(second, (), 0, SECTIONS)
    lowest = (highest + jax.random.randint(third, (), 1, SECTIONS)) % SECTIONS
    places = jnp.arange(SECTIONS)
    values = jnp.where(places == highest, TOK, jnp.where(places == lowest, TOK // 8, values))
    return values.astype(jnp.int32)


def shard_levels(stream_key, dims, cuts, smallest, high):
    loudness, own = 1.0, jax.random.fold_in(stream_key, 6)
    for axis_at, blocks in cuts:
        steps = jnp.exp(jax.random.uniform(jax.random.fold_in(own, axis_at), (blocks,), jnp.float32, smallest / len(cuts), high / len(cuts)))
        loudness = loudness * jnp.repeat(steps, dims[axis_at] // blocks).reshape([-1 if axis == axis_at else 1 for axis in range(len(dims))])
    return loudness


def centred(key, shape, deviation, most, cuts=(), kind=jnp.bfloat16):
    entries = jax.random.normal(key, shape, jnp.float32) * deviation
    if len(cuts) > 0:
        entries = shard_levels(key, shape, cuts, -0.22, 0.18) * entries
    return jnp.clip(entries, min=-most, max=most).astype(kind)


def setup_inputs(seed: int = 0) -> dict:
    key_of = jax.random.split(jax.random.key(seed), 7)
    return {
        "saved_states": draw_saved_states(jax.random.fold_in(key_of[6], 71), 0),
        "cotangent_in": centred(key_of[1], (SECTIONS, TOK, D), 1.0, 6.0, ((0, 4), (1, 8))),
        "lengths": draw_lengths(jax.random.fold_in(key_of[6], 71), 0),
        "gain": jnp.clip(1.0 + 0.18 * jax.random.normal(key_of[3], (D,), jnp.float32), 0.099609375, 1.8984375).astype(jnp.bfloat16),
        "up_weight": centred(key_of[4], (D, F), D ** -0.5, 0.125, ((0, 4), (1, 8))),
        "down_weight": centred(key_of[5], (F, D), F ** -0.5, 0.0625, ((0, 8), (1, 4))),
    }


epsilon = 1e-06

def back_iteration(state, cotangent, gain, up_weight, down_weight, with_terms):
    values = state.astype(jnp.float32)
    reciprocal = lax.rsqrt(lax.optimization_barrier(jnp.mean(values * values, axis=-1, keepdims=True)) + epsilon)
    scaled = values * reciprocal
    gain_wide = gain.astype(jnp.float32)
    normed = (scaled * gain_wide).astype(jnp.bfloat16)
    hidden_in = jnp.dot(normed, up_weight, preferred_element_type=jnp.float32)
    sigma = jax.nn.sigmoid(hidden_in)
    hidden_out = (hidden_in * sigma).astype(jnp.bfloat16)
    back_out = lax.dot_general(cotangent, down_weight, (((1,), (1,)), ((), ())), preferred_element_type=jnp.float32)
    back_in = (back_out * sigma * (1.0 + hidden_in * (1.0 - sigma))).astype(jnp.bfloat16)
    tokens = back_in.shape[0]
    blocked = back_in.astype(jnp.float32).reshape(tokens, HIDDEN_BLOCKS, -1)
    weights_blocked = up_weight.astype(jnp.float32).reshape(up_weight.shape[0], HIDDEN_BLOCKS, -1)
    partials = jnp.einsum('tgf,dgf->gtd', blocked, weights_blocked)
    rounded = lax.optimization_barrier(partials.astype(jnp.bfloat16))
    back_normed = lax.optimization_barrier(jnp.sum(rounded.astype(jnp.float32), axis=0))
    gained = back_normed * gain_wide
    back_state = reciprocal * (gained - scaled * lax.optimization_barrier(jnp.mean(gained * scaled, axis=-1, keepdims=True)))
    result = (cotangent.astype(jnp.float32) + back_state).astype(jnp.bfloat16)
    if not with_terms:
        return result
    gain_term = lax.optimization_barrier(jnp.sum(back_normed * scaled, axis=0))
    up_term = lax.dot_general(normed, back_in, (((0,), (0,)), ((), ())), preferred_element_type=jnp.float32)
    down_term = lax.dot_general(hidden_out, cotangent, (((0,), (0,)), ((), ())), preferred_element_type=jnp.float32)
    return (result, up_term, down_term, gain_term)

def reference(saved_states, cotangent_in, lengths, gain, up_weight, down_weight):
    positions = jnp.arange(TOK, dtype=jnp.int32)
    keep = positions[None, :, None] < lengths.astype(jnp.int32)[:, None, None]
    masked = jnp.where(keep, cotangent_in, jnp.zeros_like(cotangent_in))

    def carry_only(inputs):
        state, cotangent = inputs
        return back_iteration(state, cotangent, gain, up_weight, down_weight, False)
    flows = [masked]
    for turn in range(MICRO - 1):
        moved = lax.map(carry_only, (saved_states[:, turn], flows[-1]))
        flows.append(jnp.roll(moved, -1, axis=0))
    stacked = jnp.stack(flows, axis=1)
    scale = 1.0 / math.sqrt(LAP_TOKENS)

    def section_sum(carry, inputs):
        states, cotangents = inputs
        up_total, down_total, gain_total = carry
        up_section = jnp.zeros(up_weight.shape, jnp.float32)
        down_section = jnp.zeros(down_weight.shape, jnp.float32)
        result = cotangents[0]
        for turn in range(MICRO):
            result, up_term, down_term, gain_term = back_iteration(states[turn], cotangents[turn], gain, up_weight, down_weight, True)
            up_section = up_section + up_term
            down_section = down_section + down_term
            gain_total = gain_total + gain_term * scale
        up_part = lax.optimization_barrier((up_section * scale).astype(jnp.bfloat16))
        down_part = lax.optimization_barrier((down_section * scale).astype(jnp.bfloat16))
        up_total = up_total + up_part.astype(jnp.float32)
        down_total = down_total + down_part.astype(jnp.float32)
        return ((up_total, down_total, gain_total), result)
    start = (jnp.zeros(up_weight.shape, jnp.float32), jnp.zeros(down_weight.shape, jnp.float32), jnp.zeros((D,), jnp.float32))
    totals, outputs = lax.scan(section_sum, start, (saved_states, stacked))
    up_total, down_total, gain_total = totals
    return (outputs, up_total.astype(jnp.bfloat16), down_total.astype(jnp.bfloat16), gain_total)
```

```python
import math

import jax
import jax.numpy as jnp
from jax import lax
from jax.sharding import PartitionSpec as P

epsilon = 1e-06


class Ring:
    def __init__(self, axis, total, low, count):
        self.axis, self.total, self.low, self.count = axis, total, low, count
        self.binary = count & (count - 1) == 0

    def partner(self, place, k):
        if self.binary:
            return place ^ k
        return (place + k) % self.count

    def back(self, k):
        return k if self.binary else (self.count - k) % self.count

    def send(self, block, k):
        route = []
        for i in range(self.total):
            place, core = i // self.low, i % self.low
            route.append((i, self.partner(place, k) * self.low + core))
        return lax.ppermute(block, self.axis, route)

    def scatter(self, blocks):
        arrived = [blocks[0]] + [None] * (self.count - 1)
        for k in range(1, self.count):
            arrived[self.back(k)] = self.send(blocks[k], k)
        return arrived

    def gather(self, block):
        return self.scatter([block] * self.count)


def add_up(blocks):
    total = blocks[0].astype(jnp.float32)
    for block in blocks[1:]:
        total = total + block.astype(jnp.float32)
    return total


def narrow(value):
    return lax.reduce_precision(value, 8, 7)


def in_pieces(value):
    high = narrow(value)
    middle = narrow(value - high)
    low = narrow(value - high - middle)
    return [piece.astype(jnp.bfloat16) for piece in (high, middle, low)]


def dot(left, right, dims):
    return lax.dot_general(left, right, ((dims[0], dims[1]), ((), ())), preferred_element_type=jnp.float32)


def make_on_device(sections, members):
    cores = 2 if members % 2 == 0 else 1
    rows = members // cores
    plane = Ring("section", sections, 1, sections)
    line = Ring("dp", members, cores, rows)

    def other_core(block):
        return lax.ppermute(block, "dp", [(i, i ^ 1) for i in range(members)])

    def gather_members(block):
        blocks = line.gather(block)
        if cores == 2:
            blocks = blocks + [other_core(b) for b in blocks]
        stacked = jnp.stack(blocks, axis=1)
        return stacked.reshape(block.shape[0], members * block.shape[1], block.shape[2])

    def scatter_members(parts):
        tokens, width = parts[0].shape
        share = tokens // members
        whole = jnp.stack(parts, axis=0).reshape(sections, cores, rows, share, width)
        own = whole[:, 0]
        if cores == 2:
            own = add_up([own, other_core(whole[:, 1].astype(jnp.bfloat16))])
        blocks = [own[:, 0]] + [own[:, k].astype(jnp.bfloat16) for k in range(1, rows)]
        return add_up(line.scatter(blocks))

    def on_device(saved_states, cotangent_in, lengths, gain, up_weight, down_weight):
        turns, share, features = saved_states.shape[1:]
        width = up_weight.shape[0]
        here = lax.axis_index("section")
        member = lax.axis_index("dp")
        tokens = share * members
        scale = 1.0 / math.sqrt(turns * tokens * sections)

        gain_wide = gain.astype(jnp.float32)
        gain_here = lax.dynamic_index_in_dim(gain_wide.reshape(sections, width), here, 0)
        values = saved_states[0].astype(jnp.float32)
        reciprocal = lax.rsqrt(jnp.mean(values * values, axis=-1, keepdims=True) + epsilon)
        pieces = in_pieces(reciprocal)
        positions = member * share + lax.broadcasted_iota(jnp.int32, (share, 1), 0)
        own_cot = jnp.where(positions < lengths[0], cotangent_in[0], jnp.zeros_like(cotangent_in[0]))

        def slices(block):
            split = block.reshape(share, sections, -1).transpose(1, 0, 2)
            return [
                lax.dynamic_index_in_dim(split, plane.partner(here, k), 0, keepdims=False)
                for k in range(sections)
            ]

        def to_planes(block, extra=None):
            sent = slices(block)
            if extra is not None:
                sent = [jnp.concatenate([b] + extra, axis=-1) for b in sent]
            return jnp.stack(plane.scatter(sent), axis=0)

        def normalized(packed):
            wide = packed.astype(jnp.float32)
            recip = wide[..., width : width + 1] + wide[..., width + 1 : width + 2] + wide[..., width + 2 : width + 3]
            return wide[..., :width] * recip, recip

        own_states = [
            to_planes(saved_states[0, m], [piece[m] for piece in pieces]) for m in range(turns)
        ]
        cot_here = to_planes(own_cot)

        def reduced(parts):
            return add_up(plane.scatter([parts[0]] + [b.astype(jnp.bfloat16) for b in parts[1:]]))

        gain_here_total = jnp.zeros((width,), jnp.float32)
        terms = []
        for m in range(turns):
            states = gather_members(own_states[m])
            scaled, _ = normalized(states)
            normed = (scaled * gain_here).astype(jnp.bfloat16)
            hidden_in = reduced([dot(normed[k], up_weight, ((1,), (0,))) for k in range(sections)])
            cotangent = gather_members(cot_here)
            back_out = reduced([dot(cotangent[k], down_weight, ((1,), (1,))) for k in range(sections)])
            sigma = jax.nn.sigmoid(hidden_in)
            hidden_out = (hidden_in * sigma).astype(jnp.bfloat16)
            back_in = (back_out * sigma * (1.0 + hidden_in * (1.0 - sigma))).astype(jnp.bfloat16)
            all_back = plane.gather(back_in)
            back_normed = scatter_members([dot(b, up_weight, ((1,), (1,))) for b in all_back])
            all_out = plane.gather(hidden_out)
            own_scaled, own_recip = normalized(own_states[m])
            gain_here_total = gain_here_total + jnp.sum(back_normed * own_scaled, axis=(0, 1))
            terms.append((normed.reshape(-1, width), cotangent.reshape(-1, width), all_back, all_out))
            gained = back_normed * gain_here
            if m < turns - 1:
                partial = jnp.sum(gained * own_scaled, axis=-1, keepdims=True)
                mean = mean_over(plane, partial, features)
                result = cot_here.astype(jnp.float32) + own_recip * (gained - own_scaled * mean)
                result = result.astype(jnp.bfloat16)
                turned = []
                for k in range(sections):
                    source = (plane.partner(here, k) + 1) % sections
                    place = here ^ source if plane.binary else (source - here) % sections
                    turned.append(lax.dynamic_index_in_dim(result, place, 0, keepdims=False))
                cot_here = jnp.stack(turned, axis=0)
            else:
                cot_rows = in_rows(plane.scatter([cot_here[k] for k in range(sections)]), here)
                normed_rows = in_rows(
                    plane.scatter([back_normed[k].astype(jnp.bfloat16) for k in range(sections)]), here
                )
                row_scaled = values[m] * reciprocal[m]
                row_gained = normed_rows.astype(jnp.float32) * gain_wide
                state = reciprocal[m] * (
                    row_gained - row_scaled * jnp.mean(row_gained * row_scaled, axis=-1, keepdims=True)
                )
                own_rows = (cot_rows.astype(jnp.float32) + state).astype(jnp.bfloat16)[None]

        up_total = jnp.zeros(up_weight.shape, jnp.float32)
        down_total = jnp.zeros(up_weight.shape, jnp.float32)
        for normed, cotangent, all_back, all_out in terms:
            up_total = up_total + dot(normed, jnp.concatenate(all_back, axis=0), ((0,), (0,)))
            down_total = down_total + dot(cotangent, jnp.concatenate(all_out, axis=0), ((0,), (0,)))
        up_sum = (up_total * scale).astype(jnp.bfloat16)
        down_sum = (down_total * scale).astype(jnp.bfloat16).T

        part = gain_here_total * scale
        part = add_up(line.gather(part))
        if cores == 2:
            part = part + other_core(part)
        gain_sum = in_rows([b[None] for b in plane.gather(part)], here)[0]
        return (own_rows, up_sum, down_sum, gain_sum)

    def in_rows(blocks, here):
        stacked = jnp.stack(blocks, axis=0)
        ordered = []
        for d in range(sections):
            place = here ^ d if plane.binary else (d - here) % sections
            ordered.append(lax.dynamic_index_in_dim(stacked, place, 0, keepdims=False))
        return jnp.concatenate(ordered, axis=-1)

    def mean_over(ring, partial, features):
        total = partial
        for k in range(1, sections):
            arrived = ring.send(partial, k)
            moved = [arrived[j ^ k if ring.binary else (j + k) % sections] for j in range(sections)]
            total = total + jnp.stack(moved, axis=0)
        return total / features

    return on_device


def solution(mesh):
    placed = (
        P("section", None, "dp", None),
        P("section", "dp", None),
        P("section"),
        P(),
        P("section", "dp"),
        P("dp", "section"),
    )
    return jax.shard_map(
        make_on_device(mesh.shape["section"], mesh.shape["dp"]),
        mesh=mesh,
        in_specs=placed,
        out_specs=(P("section", "dp", None), P("section", "dp"), P("dp", "section"), P()),
        check_vma=False,
    )
```
